32 devices in a mesh: sub: 4 (over z), region: 8 (over y, x, core).
Axes of the slice: x: 2, y: 2, z: 4, core: 2. Of those that a mesh axis runs over, the one named last changes fastest.
Arguments:
- residual: bfloat16 [4, 8, 512, 1024], P('sub', 'region'), may hold values from -6 to 6
- send_rows: int32 [4, 8, 4, 64], P('sub', 'region'), may hold values from 0 to 511
- local_inverse: bfloat16 [4, 8, 512, 768], P('sub', 'region'), may hold values from -0.21875 to 0.21875
- coarse_basis: bfloat16 [4, 8, 512, 128], P('sub', 'region'), may hold values from -0.25 to 0.25
- regional_inverse: bfloat16 [4, 8, 128, 512], P('sub', 'region'), may hold values from -0.25 to 0.25
- root_map: bfloat16 [4, 8, 128, 64], P('sub', 'region'), may hold values from -0.75 to 0.75
- root_inverse: bfloat16 [8, 64, 512], P('region'), may hold values from -0.09375 to 0.09375
Outputs:
- correction: bfloat16 [4, 8, 512, 1024], P('sub', 'region')
The draws below stay inside these ranges and needn't reach their ends.
All inputs are finite; a program needn't handle non-finite values.
Results may differ from the reference program's by a relative error of at most 0.0055.
Values may be sent and summed in bfloat16 or wider, within the bound.
No kernel may reach another device: no remote copies, remote signals or barrier semaphores. Data moves between devices by JAX's collectives and lax.ppermute only.
A program may use at most 64 MiB of HBM per device.

```python
import jax
import jax.numpy as jnp
from jax import lax

SUBN = 768
OV = 64
KC = 128
KR = 64
C = 1024
NOWN = 512
RC = 512
ROOT = 512
N_SUB = 4
N_REGION = 8


def place_ends(drawn, rng, least, high):
    index_at = [jax.random.randint(jax.random.fold_in(rng, axis), (), 0, length) for axis, length in enumerate(drawn.shape)]
    widest = drawn.shape.index(max(drawn.shape))
    neighbour = index_at[:widest] + [(index_at[widest] + 1) % drawn.shape[widest]] + index_at[widest + 1:]
    return drawn.at[tuple(index_at)].set(least).at[tuple(neighbour)].set(high)


def levels(key, shape, split, low, top_value):
    loudness = 1.0
    for position, shards_of in split:
        heights = jax.random.uniform(jax.random.fold_in(jax.random.fold_in(key, 6), position), (shards_of,), jnp.float32, low / len(split), top_value / len(split))
        loudness = loudness * jnp.repeat(jnp.exp(heights), shape[position] // shards_of).reshape((-1,) + (1,) * (len(shape) - 1 - position))
    return loudness


def normal_values(stream_key, dims, width, most, pieces=(), kind=jnp.bfloat16):
    drawn = jax.random.normal(stream_key, dims, jnp.float32) * width
    if len(pieces) > 0:
        drawn = levels(stream_key, dims, pieces, -0.22, 0.18) * drawn
    return jnp.clip(drawn, min=-most, max=most).astype(kind)


def setup_inputs(seed: int = 0) -> dict:
    splits = jax.random.split(jax.random.key(seed), 8)
    return {
        "residual": normal_values(splits[0], (N_SUB, N_REGION, NOWN, C), 1.0, 6.0, ((0, 4), (1, 8))),
        "send_rows": place_ends(jax.random.randint(splits[1], (N_SUB, N_REGION, 4, OV), 0, NOWN), jax.random.fold_in(splits[1], 1), 0, NOWN - 1).astype(jnp.int32),
        "local_inverse": normal_values(splits[2], (N_SUB, N_REGION, NOWN, SUBN), SUBN ** -0.5, 0.21875, ((0, 4), (1, 8))),
        "coarse_basis": normal_values(splits[3], (N_SUB, N_REGION, NOWN, KC), NOWN ** -0.5, 0.25, ((0, 4), (1, 8))),
        "regional_inverse": normal_values(splits[4], (N_SUB, N_REGION, KC, RC), RC ** -0.5, 0.25, ((0, 4), (1, 8))),
        "root_map": normal_values(splits[5], (N_SUB, N_REGION, KC, KR), KR ** -0.5, 0.75, ((0, 4), (1, 8))),
        "root_inverse": normal_values(splits[6], (N_REGION, KR, ROOT), (ROOT * RC // KR) ** -0.5, 0.09375, ((0, 8),)),
    }


def pick_rows(res, idx):
    return jnp.take(res, idx, axis=0)


def reference(residual, send_rows, local_inverse, coarse_basis, regional_inverse, root_map, root_inverse):
    idx = send_rows.reshape(N_SUB, N_REGION, 4 * OV).astype(jnp.int32)
    lent = jax.vmap(jax.vmap(pick_rows))(residual, idx).reshape(N_SUB, N_REGION, 4, OV, C)
    zero_sub = jnp.zeros((1, N_REGION, OV, C), residual.dtype)
    zero_reg = jnp.zeros((N_SUB, 1, OV, C), residual.dtype)
    prev_sub = jnp.concatenate([zero_sub, lent[:-1, :, 1]], axis=0)
    next_sub = jnp.concatenate([lent[1:, :, 0], zero_sub], axis=0)
    prev_reg = jnp.concatenate([zero_reg, lent[:, :-1, 3]], axis=1)
    next_reg = jnp.concatenate([lent[:, 1:, 2], zero_reg], axis=1)

    def rhs_one(xs):
        basis, res = xs
        return jnp.einsum('gnk,gnc->gkc', basis.astype(jnp.float32), res.astype(jnp.float32)).astype(jnp.bfloat16)

    coarse_rhs = lax.map(rhs_one, (coarse_basis, residual))
    stacked = coarse_rhs.transpose(1, 0, 2, 3).reshape(N_REGION, RC, C).astype(jnp.float32)

    def regional_one(inv):
        return jnp.einsum('gkr,grc->gkc', inv.astype(jnp.float32), stacked)

    regional = lax.map(regional_one, regional_inverse)
    root_rhs = jnp.einsum('sgkr,sgkc->grc', root_map.astype(jnp.float32), coarse_rhs.astype(jnp.float32)).astype(jnp.bfloat16)
    whole = root_rhs.reshape(ROOT, C).astype(jnp.float32)
    root_sol = jnp.einsum('grq,qc->grc', root_inverse.astype(jnp.float32), whole).astype(jnp.bfloat16)
    weights = (regional + jnp.einsum('sgkr,grc->sgkc', root_map.astype(jnp.float32), root_sol.astype(jnp.float32))).astype(jnp.bfloat16)

    def final_one(xs):
        inv, res, ps, ns, pr, nr, basis, wts = xs
        vec = jnp.concatenate([res, ps, ns, pr, nr], axis=1).astype(jnp.float32)
        local = jnp.einsum('gij,gjc->gic', inv.astype(jnp.float32), vec)
        coarse = jnp.einsum('gnk,gkc->gnc', basis.astype(jnp.float32), wts.astype(jnp.float32))
        return (local + coarse).astype(jnp.bfloat16)

    return lax.map(final_one, (local_inverse, residual, prev_sub, next_sub, prev_reg, next_reg, coarse_basis, weights))
```

```python
import functools

import jax
import jax.numpy as jnp
from jax import lax
from jax.experimental import pallas as pl
from jax.experimental.pallas import tpu as pltpu
from jax.sharding import PartitionSpec as P

LANES = 128
F32 = jnp.float32
BF16 = jnp.bfloat16
VMEM = pl.BlockSpec(memory_space=pltpu.VMEM)
GRANT = 20 << 20


def xor_pairs(n, k):
    return [(i, i ^ k) for i in range(n)]


def even_pairs(n):
    up = [(i, i + 1) for i in range(0, n - 1, 2)]
    return up + [(j, i) for i, j in up]


def odd_pairs(n):
    up = [(i, i + 1) for i in range(1, n - 1, 2)]
    return up + [(j, i) for i, j in up]


def is_even(i):
    return lax.rem(i, 2) == 0


def dot(a, b):
    return jnp.dot(a, b, preferred_element_type=F32)


def dot_t(a, b):
    return lax.dot_general(a, b, (((0,), (0,)), ((), ())), preferred_element_type=F32)


def call(kernel, outs, *args, scratch=(), flops=0, name=None):
    size = sum(a.size * a.dtype.itemsize for a in args)
    size += sum(o.size * o.dtype.itemsize for o in outs)
    return pl.pallas_call(
        kernel,
        out_shape=outs,
        in_specs=[VMEM] * len(args),
        out_specs=[VMEM] * len(outs),
        scratch_shapes=list(scratch),
        cost_estimate=pl.CostEstimate(flops=flops, bytes_accessed=size, transcendentals=0),
        name=name,
        compiler_params=pltpu.CompilerParams(vmem_limit_bytes=GRANT),
    )(*args)


def shape(s, dtype):
    return jax.ShapeDtypeStruct(s, dtype)


def front_kernel(n_sub, where, res, rows, basis, root_map, rhs, ha, hb, hc, hd, *blocks):
    s, g = where[0], where[1]
    n, c = res.shape
    width = c // n_sub
    k = basis.shape[1]
    ov = rows.shape[1]
    down_s, up_s, down_g, up_g = (rows[i : i + 1, :] for i in range(4))
    even_s, even_g = is_even(s), is_even(g)
    at = lax.broadcasted_iota(jnp.int32, (n, ov), 0)
    picks = [
        jnp.where(even_s, up_s, down_s),
        jnp.where(even_s, down_s, up_s),
        jnp.where(even_g, up_g, down_g),
        jnp.where(even_g, down_g, up_g),
    ]
    hot = [jnp.where(at == p, 1.0, 0.0).astype(BF16) for p in picks]
    left = jnp.concatenate([basis[...]] + hot, axis=1)
    for j in range(n_sub):
        cols = pl.ds(j * width, width)
        both = dot_t(left, res[:, cols]).astype(BF16)
        rhs[:, cols] = both[:k]
        for i, h in enumerate((ha, hb, hc, hd)):
            h[:, cols] = both[k + i * ov : k + (i + 1) * ov]
    for i in range(n_sub):
        cols = pl.ds(pl.multiple_of((s ^ i) * width, LANES), width)
        blocks[i][...] = dot_t(root_map[...], rhs[:, cols]).astype(blocks[i].dtype)


def local_kernel(n_sub, where, inv, res, ha, hb, hc, hd, acc, halo):
    s, g = where[0], where[1]
    n, c = res.shape
    ov = ha.shape[0]
    width = c // n_sub
    even_s, even_g = is_even(s), is_even(g)
    slots = [
        jnp.where(even_s, 1, 0),
        jnp.where(even_s, 0, 1),
        jnp.where(even_g, 3, 2),
        jnp.where(even_g, 2, 3),
    ]
    for slot, h in zip(slots, (ha, hb, hc, hd)):
        halo[pl.ds(pl.multiple_of(slot * ov, ov), ov), :] = h[...]
    for j in range(n_sub):
        cols = pl.ds(j * width, width)
        acc[:, cols] = dot(inv[:, :n], res[:, cols]) + dot(inv[:, n:], halo[:, cols])


def final_kernel(n_sub, where, acc, basis, regional_rows, root_map, *rest):
    rhs, sols, out = rest[:n_sub], rest[n_sub : 2 * n_sub], rest[2 * n_sub]
    s = where[0]
    k = root_map.shape[0]
    c = acc.shape[1]
    width = c // n_sub
    for i in range(n_sub):
        cols = pl.ds(pl.multiple_of((s ^ i) * width, LANES), width)
        w = dot(root_map[...], sols[i][...])
        for j in range(n_sub):
            mine = pl.ds(pl.multiple_of((s ^ j) * k, LANES), k)
            w += dot(regional_rows[:, mine], rhs[j][:, cols])
        out[:, cols] = (acc[:, cols] + dot(basis[...], w.astype(BF16))).astype(BF16)


def root_kernel(n_pairs, where, root_rows, *rest):
    parts, out = rest[:n_pairs], rest[n_pairs]
    g = where[1]
    depth = parts[0].shape[0]
    total = None
    for i in range(n_pairs):
        at = pl.ds(pl.multiple_of((lax.div(g, 2) ^ i) * depth, LANES), depth)
        term = dot(root_rows[:, at], parts[i][...])
        total = term if total is None else total + term
    out[...] = total.astype(out.dtype)


def smem_call(kernel, outs, where, *args, scratch=(), flops=0, name=None):
    size = sum(a.size * a.dtype.itemsize for a in args)
    size += sum(o.size * o.dtype.itemsize for o in outs)
    return pl.pallas_call(
        kernel,
        out_shape=outs,
        in_specs=[pl.BlockSpec(memory_space=pltpu.SMEM)] + [VMEM] * len(args),
        out_specs=[VMEM] * len(outs),
        scratch_shapes=list(scratch),
        cost_estimate=pl.CostEstimate(flops=flops, bytes_accessed=size, transcendentals=0),
        name=name,
        compiler_params=pltpu.CompilerParams(vmem_limit_bytes=GRANT),
    )(where, *args)


def per_device(
    residual, send_rows, local_inverse, coarse_basis, regional_inverse, root_map, root_inverse
):
    n_sub, n_reg = lax.axis_size("sub"), lax.axis_size("region")
    res, rows, inv = residual[0, 0], send_rows[0, 0], local_inverse[0, 0]
    basis, reg_rows, to_root, root_rows = (
        coarse_basis[0, 0], regional_inverse[0, 0], root_map[0, 0], root_inverse[0],
    )
    n, c = res.shape
    ov, k, kr = rows.shape[1], basis.shape[1], to_root.shape[1]
    width = c // n_sub
    s, g = lax.axis_index("sub"), lax.axis_index("region")
    where = jnp.stack([s, g]).astype(jnp.int32)

    outs = smem_call(
        functools.partial(front_kernel, n_sub),
        [shape((k, c), BF16)] + [shape((ov, c), BF16)] * 4 + [shape((kr, width), BF16)] * n_sub,
        where, res, rows, basis, to_root,
        flops=2 * n * c * (k + 4 * ov), name="front",
    )
    rhs, halo, parts = outs[0], outs[1:5], outs[5:]

    got = [parts[0]] + [
        lax.ppermute(parts[i], "sub", xor_pairs(n_sub, i)) for i in range(1, n_sub)
    ]
    mine = sum(p.astype(F32) for p in got).astype(BF16)
    theirs = lax.ppermute(mine, "region", xor_pairs(n_reg, 1))
    even = is_even(g)
    pair = jnp.concatenate([jnp.where(even, mine, theirs), jnp.where(even, theirs, mine)], axis=0)
    pairs = [pair] + [
        lax.ppermute(pair, "region", xor_pairs(n_reg, 2 * i)) for i in range(1, n_reg // 2)
    ]
    (sol,) = smem_call(
        functools.partial(root_kernel, n_reg // 2),
        [shape((kr, width), BF16)], where, root_rows, *pairs, name="root",
    )
    sols = [sol] + [lax.ppermute(sol, "sub", xor_pairs(n_sub, i)) for i in range(1, n_sub)]

    all_rhs = [rhs] + [lax.ppermute(rhs, "sub", xor_pairs(n_sub, i)) for i in range(1, n_sub)]
    ha = lax.ppermute(halo[0], "sub", even_pairs(n_sub))
    hb = lax.ppermute(halo[1], "sub", odd_pairs(n_sub))
    hc = lax.ppermute(halo[2], "region", even_pairs(n_reg))
    hd = lax.ppermute(halo[3], "region", odd_pairs(n_reg))
    (acc,) = smem_call(
        functools.partial(local_kernel, n_sub),
        [shape((n, c), F32)], where, inv, res, ha, hb, hc, hd,
        scratch=[pltpu.VMEM((4 * ov, c), BF16)], flops=2 * n * c * (n + 4 * ov), name="local",
    )
    (out,) = smem_call(
        functools.partial(final_kernel, n_sub),
        [shape((n, c), BF16)], where, acc, basis, reg_rows, to_root, *all_rhs, *sols,
        flops=2 * n * c * k, name="final",
    )
    return out.reshape(1, 1, n, c)


def solution(mesh):
    grid = P("sub", "region", None, None)
    return jax.shard_map(
        per_device, mesh=mesh, in_specs=(grid,) * 6 + (P("region", None, None),),
        out_specs=grid, check_vma=False,
    )
```

```python
import functools

import jax
import jax.numpy as jnp
from jax import lax
from jax.experimental import pallas as pl
from jax.experimental.pallas import tpu as pltpu
from jax.sharding import PartitionSpec as P

LANES = 128
F32 = jnp.float32
BF16 = jnp.bfloat16
VMEM = pl.BlockSpec(memory_space=pltpu.VMEM)
HBM = pl.BlockSpec(memory_space=pltpu.HBM)
SMEM = pl.BlockSpec(memory_space=pltpu.SMEM)
GRANT = 12 << 20


def xor_pairs(n, k):
    return [(i, i ^ k) for i in range(n)]


def even_pairs(n):
    up = [(i, i + 1) for i in range(0, n - 1, 2)]
    return up + [(j, i) for i, j in up]


def odd_pairs(n):
    up = [(i, i + 1) for i in range(1, n - 1, 2)]
    return up + [(j, i) for i, j in up]


def is_even(i):
    return lax.rem(i, 2) == 0


def dot(a, b):
    return jnp.dot(a, b, preferred_element_type=F32)


def dot_t(a, b):
    return lax.dot_general(a, b, (((0,), (0,)), ((), ())), preferred_element_type=F32)


def shape(s, dtype):
    return jax.ShapeDtypeStruct(s, dtype)


def call(kernel, outs, in_specs, args, scratch=(), out_specs=None, flops=0):
    size = sum(a.size * a.dtype.itemsize for a in args)
    size += sum(o.size * o.dtype.itemsize for o in outs)
    return pl.pallas_call(
        kernel,
        out_shape=outs,
        in_specs=in_specs,
        out_specs=out_specs or [VMEM] * len(outs),
        scratch_shapes=list(scratch),
        cost_estimate=pl.CostEstimate(flops=flops, bytes_accessed=size, transcendentals=0),
        compiler_params=pltpu.CompilerParams(vmem_limit_bytes=GRANT),
    )(*args)


def front_kernel(n_sub, res_h, basis_h, map_h, reg_h, inv_h, rows_h, *refs):
    res, basis, to_root, reg, inv, rows, rhs = refs[:7]
    blocks, sems = refs[7 : 7 + n_sub], refs[7 + n_sub]
    s = lax.axis_index("sub")
    c = res.shape[1]
    width = c // n_sub
    k, kr = basis.shape[1], to_root.shape[0]
    pairs = ((basis_h, basis), (map_h, to_root), (reg_h, reg), (inv_h, inv), (rows_h, rows))
    small = [pltpu.make_async_copy(x, y, sems.at[n_sub + i]) for i, (x, y) in enumerate(pairs)]
    loads = [
        pltpu.make_async_copy(
            res_h.at[:, pl.ds(j * width, width)], res.at[:, pl.ds(j * width, width)], sems.at[j]
        )
        for j in range(n_sub)
    ]
    for copy in small[:1] + loads + small[1:]:
        copy.start()
    small[0].wait()
    for j in range(n_sub):
        loads[j].wait()
        cols = pl.ds(j * width, width)
        rhs[:, cols] = dot_t(basis[...], res[:, cols]).astype(BF16)
    for copy in small[1:]:
        copy.wait()
    for i in range(n_sub):
        cols = pl.ds(pl.multiple_of((s ^ i) * width, LANES), width)
        blocks[i][:kr, :] = dot(to_root[...], rhs[:, cols]).astype(BF16)
    for j in (2, 3):
        mine = pl.ds(pl.multiple_of((s ^ j) * k, LANES), k)
        blocks[1][kr:, (j - 2) * k : (j - 1) * k] = reg[:, mine]


def lent_kernel(n_sub, rows, res, rhs, even, hb, hc, hd):
    s, g = lax.axis_index("sub"), lax.axis_index("region")
    n, c = res.shape
    width = c // n_sub
    k, ov = rhs.shape[0], rows.shape[1]
    even_s, even_g = is_even(s), is_even(g)
    down_s, up_s, down_g, up_g = (rows[i : i + 1, :] for i in range(4))
    at = lax.broadcasted_iota(jnp.int32, (n, ov), 0)
    picks = [
        jnp.where(even_s, up_s, down_s),
        jnp.where(even_s, down_s, up_s),
        jnp.where(even_g, up_g, down_g),
        jnp.where(even_g, down_g, up_g),
    ]
    hot = jnp.concatenate([jnp.where(at == p, 1.0, 0.0).astype(BF16) for p in picks], axis=1)
    for j in range(n_sub):
        cols = pl.ds(j * width, width)
        lent = dot_t(hot, res[:, cols]).astype(BF16)
        even[:k, cols] = rhs[:, cols]
        even[k:, cols] = lent[:ov]
        hb[:, cols] = lent[ov : 2 * ov]
        hc[:, cols] = lent[2 * ov : 3 * ov]
        hd[:, cols] = lent[3 * ov :]


def partial_kernel(with_rows, odd, far, out):
    k = far.shape[0]
    left = with_rows[with_rows.shape[0] - k :, :]
    out[...] = (dot(left[:, :k], odd[...]) + dot(left[:, k:], far[...])).astype(BF16)


def local_kernel(n_sub, inv, res, basis, reg, rhs, even, far, odd, hb, hc, hd, acc, halo):
    s, g = lax.axis_index("sub"), lax.axis_index("region")
    n, c = res.shape
    k, ov = rhs.shape[0], hb.shape[0]
    width = c // n_sub
    even_s, even_g = is_even(s), is_even(g)
    slots = [
        jnp.where(even_s, 1, 0),
        jnp.where(even_s, 0, 1),
        jnp.where(even_g, 3, 2),
        jnp.where(even_g, 2, 3),
    ]
    lent = (even[k : k + ov, :], hb[...], hc[...], hd[...])
    for slot, h in zip(slots, lent):
        halo[pl.ds(pl.multiple_of(slot * ov, ov), ov), :] = h
    for j in range(n_sub):
        cols = pl.ds(j * width, width)
        w = None
        for i, r in enumerate((rhs, even, far, odd)):
            mine = pl.ds(pl.multiple_of((s ^ i) * k, LANES), k)
            term = dot(reg[:, mine], r[:k, cols])
            w = term if w is None else w + term
        acc[:, cols] = (
            dot(inv[:, :n], res[:, cols]) + dot(inv[:, n:], halo[:, cols])
            + dot(basis[...], w.astype(BF16))
        )


def final_kernel(n_sub, steps, acc, basis, to_root, nxt, *rest):
    sols, (out_h, out, weights, sems) = rest[:n_sub], rest[n_sub:]
    s = lax.axis_index("sub")
    n, c = acc.shape
    width = c // n_sub
    for i in range(n_sub):
        cols = pl.ds(pl.multiple_of((s ^ i) * width, LANES), width)
        w = dot_t(to_root[...], sols[i][...]) + nxt[:, cols].astype(F32)
        weights[:, cols] = w.astype(BF16)
    copies = []
    for i in range(steps):
        rows = pl.ds(i * (n // steps), n // steps)
        out[rows, :] = (acc[rows, :] + dot(basis[rows, :], weights[...])).astype(BF16)
        copy = pltpu.make_async_copy(out.at[rows, :], out_h.at[rows, :], sems.at[i])
        copy.start()
        copies.append(copy)
    for copy in copies:
        copy.wait()


def sum_kernel(*refs):
    rows = refs[0].shape[0]
    total = refs[0][...].astype(F32)
    for r in refs[1:-1]:
        total += r[:rows, :].astype(F32)
    refs[-1][...] = total.astype(BF16)


def pair_kernel(mine, theirs, out):
    rows = mine.shape[0]
    odd = lax.rem(lax.axis_index("region"), 2)
    out[pl.ds(pl.multiple_of(odd * rows, rows), rows), :] = mine[...]
    out[pl.ds(pl.multiple_of((1 - odd) * rows, rows), rows), :] = theirs[...]


def root_kernel(n_pairs, root_rows, *rest):
    parts, out = rest[:n_pairs], rest[n_pairs]
    g = lax.axis_index("region")
    depth = parts[0].shape[0]
    total = None
    for i in range(n_pairs):
        at = pl.ds(pl.multiple_of((lax.div(g, 2) ^ i) * depth, LANES), depth)
        term = dot(root_rows[:, at], parts[i][...])
        total = term if total is None else total + term
    out[...] = total.astype(out.dtype)


def per_device(
    residual, send_rows, local_inverse, coarse_basis, regional_inverse, root_map, root_inverse
):
    n_sub, n_reg = lax.axis_size("sub"), lax.axis_size("region")
    res, rows, inv = residual[0, 0], send_rows[0, 0], local_inverse[0, 0]
    basis, reg_rows, to_root, root_rows = (
        coarse_basis[0, 0], regional_inverse[0, 0], root_map[0, 0].T, root_inverse[0],
    )
    n, c = res.shape
    ov, k, kr = rows.shape[1], basis.shape[1], to_root.shape[0]
    width = c // n_sub

    loaded = (res, basis, to_root, reg_rows, root_rows, rows)
    outs = call(
        functools.partial(front_kernel, n_sub),
        [shape(a.shape, a.dtype) for a in loaded] + [shape((k, c), BF16)]
        + [shape((kr + k if i == 1 else kr, width), BF16) for i in range(n_sub)],
        [HBM] * 6, tuple(pltpu.with_memory_space_constraint(a, pltpu.HBM) for a in loaded),
        scratch=[pltpu.SemaphoreType.DMA((n_sub + 5,))], flops=2 * n * c * k,
    )
    res, basis, to_root, reg_rows, root_rows, rows, rhs = outs[:7]
    parts = outs[7:]
    to_even, to_hb, to_hc, to_hd = call(
        functools.partial(lent_kernel, n_sub),
        [shape((k + ov, c), BF16)] + [shape((ov, c), BF16)] * 3,
        [VMEM] * 3, (rows, res, rhs), flops=8 * n * c * ov,
    )

    got = [parts[0]] + [lax.ppermute(parts[i], "sub", xor_pairs(n_sub, i)) for i in range(1, n_sub)]
    far = lax.ppermute(rhs, "sub", [(0, 2), (3, 1)])
    odd = lax.ppermute(rhs, "sub", odd_pairs(n_sub))
    hb = lax.ppermute(to_hb, "sub", odd_pairs(n_sub))
    even = lax.ppermute(to_even, "sub", even_pairs(n_sub))
    hc = lax.ppermute(to_hc, "region", even_pairs(n_reg))
    hd = lax.ppermute(to_hd, "region", odd_pairs(n_reg))

    (mine,) = call(sum_kernel, [shape((kr, width), BF16)], [VMEM] * n_sub, tuple(got))
    theirs = lax.ppermute(mine, "region", xor_pairs(n_reg, 1))
    (pair,) = call(pair_kernel, [shape((2 * kr, width), BF16)], [VMEM] * 2, (mine, theirs))
    pairs = [pair] + [
        lax.ppermute(pair, "region", xor_pairs(n_reg, 2 * i)) for i in range(1, n_reg // 2)
    ]
    (sol,) = call(
        functools.partial(root_kernel, n_reg // 2),
        [shape((kr, width), BF16)], [VMEM] * (1 + n_reg // 2), (root_rows, *pairs),
    )
    sols = [sol] + [lax.ppermute(sol, "sub", xor_pairs(n_sub, i)) for i in range(1, n_sub)]
    (partial,) = call(
        partial_kernel, [shape((k, c), BF16)], [VMEM] * 3, (got[1], odd, far),
        flops=4 * k * k * c,
    )
    nxt = lax.ppermute(partial, "sub", even_pairs(n_sub))

    (acc,) = call(
        functools.partial(local_kernel, n_sub),
        [shape((n, c), F32)], [VMEM] * 11,
        (inv, res, basis, reg_rows, rhs, even, far, odd, hb, hc, hd),
        scratch=[pltpu.VMEM((4 * ov, c), BF16)], flops=2 * n * c * (n + 4 * ov + 2 * k),
    )
    steps = 4
    (out,) = call(
        functools.partial(final_kernel, n_sub, steps),
        [shape((n, c), BF16)], [VMEM] * (4 + n_sub), (acc, basis, to_root, nxt, *sols),
        scratch=[
            pltpu.VMEM((n, c), BF16), pltpu.VMEM((k, c), BF16), pltpu.SemaphoreType.DMA((steps,)),
        ],
        out_specs=[HBM], flops=2 * n * c * k,
    )
    return out.reshape(1, 1, n, c)


def shifted(x, axis, step):
    n = lax.axis_size(axis)
    return lax.ppermute(x, axis, [(i, i + step) for i in range(n) if 0 <= i + step < n])


def any_size(
    residual, send_rows, local_inverse, coarse_basis, regional_inverse, root_map, root_inverse
):
    owned, rows = residual[0, 0], send_rows[0, 0]
    basis, part = coarse_basis[0, 0], root_map[0, 0]
    n, c = owned.shape
    lent = jnp.take(owned, rows.reshape(-1), axis=0).reshape(4, rows.shape[1], c)
    moves = (("sub", 1, 1), ("sub", -1, 0), ("region", 1, 3), ("region", -1, 2))
    halo = [shifted(lent[i], axis, step) for axis, step, i in moves]
    local = dot(local_inverse[0, 0], jnp.concatenate([owned] + halo, axis=0))
    rhs = dot_t(basis, owned).astype(BF16)
    regional = dot(regional_inverse[0, 0], lax.all_gather(rhs, "sub", axis=0, tiled=True))
    block = lax.psum_scatter(dot_t(part, rhs), "sub", scatter_dimension=1, tiled=True)
    whole = lax.all_gather(block.astype(BF16), "region", axis=0, tiled=True)
    sol = lax.all_gather(dot(root_inverse[0], whole).astype(BF16), "sub", axis=1, tiled=True)
    weights = (regional + dot(part, sol)).astype(BF16)
    return (local + dot(basis, weights)).astype(BF16).reshape(1, 1, n, c)


def solution(mesh):
    grid = P("sub", "region", None, None)
    n_sub, n_reg = mesh.shape["sub"], mesh.shape["region"]
    short = n_sub == 4 and n_reg % 2 == 0

    def body(*args):
        width, k = args[0].shape[3] // n_sub, args[3].shape[3]
        if not short or width != 2 * k or k % LANES:
            return any_size(*args)
        return per_device(*args)

    return jax.shard_map(
        body, mesh=mesh, in_specs=(grid,) * 6 + (P("region", None, None),),
        out_specs=grid, check_vma=False,
    )
```
